32 devices in a mesh: row: 4 (over z), col: 4 (over y, x), vec: 2 (over core).
Axes of the slice: x: 2, y: 2, z: 4, core: 2. Of those that a mesh axis runs over, the one named last changes fastest.
Arguments:
- vectors: bfloat16 [8, 32768], P('vec', 'row'), may hold values from -6 to 6
- energy: float32 [32768], P('row'), may hold values from 1 to 10
- tiles: bfloat16 [4, 4, 192, 4096], P('row', 'col'), may hold values from -0.30618622 to 0.30618622
- tile_rows: int32 [4, 4, 192], P('row', 'col'), may hold values from 0 to 127
- tile_cols: int32 [4, 4, 192], P('row', 'col'), may hold values from 0 to 127
- counts: int32 [4, 4], P('row', 'col'), may hold values from 48 to 192, as said below
Outputs:
- image: float32 [8, 32768], P('vec', 'row')
- residual_image: float32 [8, 32768], P('vec', 'row')
The draws below stay inside these ranges and needn't reach their ends.
Inputs may be any that keep to these rules, and one draw needn't show every extreme that they name: `counts`: at least one block has all 192 slots live in every draw; slots at or past a block's count hold no part of H.
All inputs are finite; a program needn't handle non-finite values.
Results may differ from the reference program's by a relative error of at most 0.004.
Values may be sent and summed in bfloat16 or wider, within the bound.
A program may use at most 64 MiB of HBM per device.

```python
import math
import jax
import jax.numpy as jnp
from jax import lax

K = 8
GB = 128
MAXT = 192
GROUPS = 4
D = 32768
FAN = 384


def draw_counts(key, part):
    first = jax.random.fold_in(key, 17)
    second = jax.random.fold_in(key, 29)
    values = jax.random.randint(first, (GROUPS * GROUPS,), MAXT // 4, MAXT + 1)
    chosen = jax.random.randint(second, (), 0, GROUPS * GROUPS)
    values = jnp.where(jnp.arange(GROUPS * GROUPS) == chosen, MAXT, values)
    return values.reshape(GROUPS, GROUPS).astype(jnp.int32)


def draw_vectors(key, part):
    position = jnp.arange(D, dtype=jnp.float32) / D
    noise = jnp.clip(jax.random.normal(key, (K, D), jnp.float32), -4.5, 4.5)
    offset = 0.5 * (0.5 + position)
    return (noise + offset[None, :]).astype(jnp.bfloat16)


def draw_tiles(key, part):
    shape = (GROUPS, GROUPS, MAXT, 4096)
    spread = FAN ** (-0.5)
    noise = jnp.clip(jax.random.normal(key, shape, jnp.float32), -5.0, 5.0)
    offset = 1.0 / FAN
    return (noise * spread + offset).astype(jnp.bfloat16)


def touch_ends(result, rng, least, largest):
    longest = result.shape.index(max(result.shape))
    spots = []
    for shift in (0, 1):
        where = [jax.random.randint(jax.random.fold_in(rng, axis), (), 0, length) for axis, length in enumerate(result.shape)]
        where[longest] = (where[longest] + shift) % result.shape[longest]
        spots.append(tuple(where))
    return result.at[spots[0]].set(least).at[spots[1]].set(largest)


def levels(stream_key, dims, cuts, smallest, high):
    def one(axis_at, parts):
        heights = jax.random.uniform(jax.random.fold_in(jax.random.fold_in(stream_key, 6), axis_at), (parts,), jnp.float32, smallest / len(cuts), high / len(cuts))
        return jnp.repeat(jnp.exp(heights), dims[axis_at] // parts).reshape((-1,) + (1,) * (len(dims) - axis_at - 1))

    gain = one(*cuts[0])
    for cut in cuts[1:]:
        gain = gain * one(*cut)
    return gain


def setup_inputs(seed: int = 0) -> dict:
    seeds = jax.random.split(jax.random.key(seed), 7)
    vectors = draw_vectors(jax.random.fold_in(seeds[6], 71), 0)
    energy = jnp.clip(jnp.exp(math.log(10.0) - 2.3025851 * jax.random.uniform(seeds[1], (D,), jnp.float32) ** levels(seeds[1], (D,), ((0, 4),), -0.2, 0.2)), 1.0, 10.0)
    tiles = draw_tiles(jax.random.fold_in(seeds[6], 71), 0)
    tile_rows = touch_ends(jax.random.randint(seeds[3], (GROUPS, GROUPS, MAXT), 0, GB), jax.random.fold_in(seeds[3], 1), 0, GB - 1).astype(jnp.int32)
    tile_cols = touch_ends(jax.random.randint(seeds[4], (GROUPS, GROUPS, MAXT), 0, GB), jax.random.fold_in(seeds[4], 1), 0, GB - 1).astype(jnp.int32)
    counts = draw_counts(jax.random.fold_in(seeds[6], 71), 0)
    return dict(vectors=vectors, energy=energy, tiles=tiles, tile_rows=tile_rows, tile_cols=tile_cols, counts=counts)


def apply_hamiltonian(block, tiles, tile_rows, tile_cols, counts, energy):
    vectors_here = block.shape[0]
    grid = block.astype(jnp.float32).reshape(vectors_here, GROUPS * GB, 64)

    def visit(total, index):
        group_row = index // GROUPS
        group_col = index % GROUPS
        square = tiles[group_row, group_col].astype(jnp.float32).reshape(MAXT, 64, 64)
        rows = (group_row * GB + tile_rows[group_row, group_col]).astype(jnp.int32)
        cols = (group_col * GB + tile_cols[group_row, group_col]).astype(jnp.int32)
        live = (jnp.arange(MAXT) < counts[group_row, group_col]).astype(jnp.float32)
        forward = jnp.einsum('tab,ktb->kta', square, grid[:, cols, :], precision=lax.Precision.HIGHEST) * live[None, :, None]
        backward = jnp.einsum('tab,kta->ktb', square, grid[:, rows, :], precision=lax.Precision.HIGHEST) * live[None, :, None]
        total = total.at[:, rows, :].add(forward)
        total = total.at[:, cols, :].add(backward)
        return total, None

    start = jnp.zeros((vectors_here, GROUPS * GB, 64), jnp.float32)
    total, _ = lax.scan(visit, start, jnp.arange(GROUPS * GROUPS, dtype=jnp.int32))
    return total.reshape(vectors_here, -1) + energy[None, :] * block.astype(jnp.float32)


def reference(vectors, energy, tiles, tile_rows, tile_cols, counts):
    image = apply_hamiltonian(vectors, tiles, tile_rows, tile_cols, counts, energy)
    widened = vectors.astype(jnp.float32)
    theta = jnp.sum(widened * image, axis=1) / jnp.sum(widened * widened, axis=1)
    residual = (image - theta[:, None] * widened).astype(jnp.bfloat16)
    residual_image = apply_hamiltonian(residual, tiles, tile_rows, tile_cols, counts, energy)
    return image, residual_image
```

```python
import functools

import jax
import jax.numpy as jnp
from jax import lax
from jax.experimental import pallas as pl
from jax.experimental.pallas import tpu as pltpu
from jax.sharding import PartitionSpec as P

F32 = jnp.float32
BF16 = jnp.bfloat16
SIDE = 64
LANES = 128


def kernel(
    n, counts_ref, raw_any, e_any, rows_any, cols_any, t_any, image_out, second_out,
    raw_ref, e_ref, t_ref, rows_ref, cols_ref, v_ref, wide, final, spread_mat, low_mat, high_mat, prods, acc, near, far, row_part, row_stage, col_stage,
    row_in, col_in, num_out, num_in, far_send, far_recv, near_send, near_recv, row_send,
    row_recv, col_send, col_recv, num_send, num_recv, out_send, out_recv, load_sem,
):
    r, c = lax.axis_index("row"), lax.axis_index("col")
    me = r * n + c
    everyone = n * n
    pieces, depth, width = v_ref.shape
    groups = pieces * depth
    pairs = width // LANES
    slots, area = t_ref.shape
    diagonal = r == c

    def copy(src, dst, send, recv, row, col):
        return pltpu.make_async_remote_copy(
            src_ref=src, dst_ref=dst, send_sem=send, recv_sem=recv,
            device_id={"row": row, "col": col}, device_id_type=pl.DeviceIdType.MESH,
        )

    def each(start, stop, body):
        def step(i, carry):
            body(i)
            return carry

        lax.fori_loop(start, stop, step, 0)

    def far_copy(src, phase, shift):
        return copy(
            src, far.at[phase, c], far_send.at[phase, shift - 1], far_recv.at[phase, c],
            lax.rem(r + shift, n), r,
        )

    def far_wait(phase):
        @pl.when(jnp.logical_not(diagonal))
        def _():
            each(0, n, lambda q: copy(
                near.at[q], far.at[phase, q], far_send.at[phase, 0], far_recv.at[phase, q], r, c
            ).wait_recv())

    def row_copy(phase, shift):
        q = lax.rem(c + shift, n)
        return copy(
            row_stage.at[phase, q], row_in.at[phase, c], row_send.at[phase, shift - 1],
            row_recv.at[phase, c], r, q,
        )

    def col_copy(phase, q):
        return copy(
            col_stage.at[phase, q], col_in.at[phase, r], col_send.at[phase, q],
            col_recv.at[phase, r], c, q,
        )

    def not_me(q, body):
        @pl.when(jnp.logical_not(jnp.logical_and(diagonal, q == c)))
        def _():
            body()

    def near_copy(shift):
        return copy(
            near.at[c], near.at[c], near_send.at[shift - 1], near_recv.at[c],
            r, lax.rem(c + shift, n),
        )

    block_rows = final.shape[1]

    def lines(ref, q):
        return ref.at[pl.ds(pl.multiple_of(q * block_rows, block_rows), block_rows), :]

    def out_copy(phase, ref, shift):
        return copy(
            final.at[phase], lines(ref, c), out_send.at[phase, shift - 1],
            out_recv.at[phase, c], r, lax.rem(c + shift, n),
        )

    def num_copy(shift):
        peer = lax.rem(me + shift, everyone)
        return copy(
            num_out, num_in.at[me], num_send.at[shift - 1], num_recv.at[me],
            peer // n, lax.rem(peer, n),
        )

    barrier = pltpu.get_barrier_semaphore()

    def greet(shift):
        peer = lax.rem(me + shift, everyone)
        pl.semaphore_signal(
            barrier, inc=1, device_id={"row": peer // n, "col": lax.rem(peer, n)},
            device_id_type=pl.DeviceIdType.MESH,
        )

    loads = [
        pltpu.make_async_copy(src, dst, load_sem.at[i])
        for i, (src, dst) in enumerate(
            (
                (raw_any, raw_ref), (e_any, e_ref), (rows_any, rows_ref), (cols_any, cols_ref),
                (t_any, t_ref),
            )
        )
    ]
    for load in loads:
        load.start()
    each(1, everyone, greet)

    for load in loads[:2]:
        load.wait()
    here = width // SIDE
    half_rows = groups // 2
    half = depth // 2

    def pack(parts):
        out = []
        for p in range(len(parts) // 2):
            first, second = parts[2 * p], parts[2 * p + 1]
            mask = lax.broadcasted_iota(jnp.int32, first.shape, 1) < SIDE
            out.append((
                jnp.where(mask, first, pltpu.roll(second, SIDE, 1)),
                jnp.where(mask, pltpu.roll(first, SIDE, 1), second),
            ))
        return out

    wide[...] = raw_ref[...].astype(F32)
    packed = pack([wide[pl.ds(k, half_rows, stride=here), :] for k in range(here)])
    for p in range(pairs):
        for parity in range(2):
            for q in range(pieces):
                v_ref[q, half * parity: half * (parity + 1), LANES * p: LANES * (p + 1)] = (
                    packed[p][parity][half * q: half * (q + 1)].astype(BF16)
                )
    energies = e_ref[pl.ds(pl.multiple_of(c * half, half), half), :]
    ((upper_energy, lower_energy),) = pack([energies, energies])
    energy = jnp.concatenate(
        [jnp.concatenate([upper_energy, lower_energy], axis=0)] * pairs, axis=1
    )

    shift = SIDE.bit_length() - 1
    owner = lax.shift_right_logical(lax.broadcasted_iota(jnp.int32, low_mat.shape, 1), shift)
    line = lax.broadcasted_iota(jnp.int32, low_mat.shape, 0)
    low_mat[...] = (owner == line).astype(BF16)
    high_mat[...] = (owner + SIDE == line).astype(BF16)

    for load in loads[2:]:
        load.wait()

    live = lax.broadcasted_iota(jnp.int32, (groups, slots), 1) < counts_ref[0, 0]
    place = lax.broadcasted_iota(jnp.int32, (groups, slots), 0)

    def home(index):
        inside = jnp.bitwise_and(index, depth - 1)
        return index - inside + half * jnp.bitwise_and(index, 1) + lax.shift_right_logical(inside, 1)

    pick_rows = jnp.where(
        jnp.logical_and(place == home(rows_ref[...]), live), 1.0, 0.0
    ).astype(BF16)
    pick_cols = jnp.where(
        jnp.logical_and(place == home(cols_ref[...]), live), 1.0, 0.0
    ).astype(BF16)
    left = lax.broadcasted_iota(jnp.int32, (slots, LANES), 1) < SIDE

    def whole(value):
        return value.astype(F32).reshape(groups, width).astype(BF16)

    def fetch(pick, value):
        return lax.dot_general(
            pick, whole(value), (((0,), (0,)), ((), ())), preferred_element_type=F32
        )

    def deposit(pick, value):
        upper = value.astype(BF16)
        lower = (value - upper.astype(F32)).astype(BF16)
        total = jnp.dot(pick, upper, preferred_element_type=F32) + jnp.dot(
            pick, lower, preferred_element_type=F32
        )
        return total.reshape(pieces, depth, width)

    def backward(own):
        mine = fetch(pick_rows, own)
        stacked = jnp.concatenate(
            [mine[:, LANES * p: LANES * (p + 1)] for p in range(pairs)], axis=0
        ).astype(BF16)
        acc[...] = jnp.zeros_like(acc)
        chunk = 4 * LANES

        def step(i, carry):
            at = pl.ds(pl.multiple_of(i * chunk, chunk), chunk)
            tile = t_ref[:, at].astype(F32)
            for half, mat in enumerate((low_mat, high_mat)):
                wide = jnp.dot(stacked, mat[:, at], preferred_element_type=F32)
                for p in range(pairs):
                    prod = wide[slots * p: slots * (p + 1)] * tile
                    part = prod[:, :LANES]
                    for j in range(1, chunk // LANES):
                        part = part + prod[:, LANES * j: LANES * (j + 1)]
                    acc[2 * p + half] += part
            return carry

        lax.fori_loop(0, area // chunk, step, 0, unroll=2)
        parts = []
        for p in range(pairs):
            first, second = acc[2 * p], acc[2 * p + 1]
            parts.append(jnp.where(
                left, first + pltpu.roll(first, SIDE, 1), second + pltpu.roll(second, SIDE, 1)
            ))
        return jnp.concatenate(parts, axis=1)

    def forward(theirs):
        twins = []
        for p in range(pairs):
            both = theirs[:, LANES * p: LANES * (p + 1)]
            turned = pltpu.roll(both, SIDE, 1)
            for twin in (jnp.where(left, both, turned), jnp.where(left, turned, both)):
                twins.append(jnp.concatenate([twin.astype(BF16)] * 8, axis=1))

        chunk = 8 * LANES
        prods[...] = jnp.zeros_like(prods)

        def step(i, carry):
            base = pl.multiple_of(i * chunk, chunk)
            tile = t_ref[:, pl.ds(base, chunk)]
            total = None
            for half in range(2):
                left_side = jnp.concatenate(
                    [tile * twins[2 * p + half] for p in range(pairs)], axis=0
                )
                start = pl.multiple_of(base + half * area, chunk)
                part = jnp.dot(
                    left_side, spread_mat[pl.ds(start, chunk), :], preferred_element_type=F32
                )
                total = part if total is None else total + part
            prods[...] += total
            return carry

        lax.fori_loop(0, area // chunk, step, 0, unroll=2)
        summed = prods[...]
        return jnp.concatenate(
            [summed[slots * p: slots * (p + 1)] for p in range(pairs)], axis=1
        )

    def scatter_col(phase, part):
        col_stage[phase] = part.astype(BF16)
        each(0, n, lambda q: not_me(q, lambda: col_copy(phase, q).start()))

        @pl.when(diagonal)
        def _():
            col_in[phase, r] = col_stage[phase, c]

    def scatter_row(phase, part):
        row_part[...] = part
        row_stage[phase] = part.astype(BF16)
        each(1, n, lambda s: row_copy(phase, s).start())

    def gathered(phase, start):
        def row_step(s, carry):
            q = lax.rem(c + s, n)
            copy(
                row_stage.at[phase, 0], row_in.at[phase, q], row_send.at[phase, 0],
                row_recv.at[phase, q], r, q,
            ).wait_recv()
            return carry + row_in[phase, q].astype(F32)

        total = lax.fori_loop(1, n, row_step, start + row_part[c])

        def col_step(q, carry):
            @pl.when(jnp.logical_not(jnp.logical_and(diagonal, q == r)))
            def _():
                copy(
                    col_stage.at[phase, 0], col_in.at[phase, q], col_send.at[phase, 0],
                    col_recv.at[phase, q], q, r,
                ).wait_recv()

            return carry + col_in[phase, q].astype(F32)

        return lax.fori_loop(0, n, col_step, total)

    pl.semaphore_wait(barrier, everyone - 1)
    each(1, n, lambda s: far_copy(v_ref.at[c], 0, s).start())
    sums_back = backward(v_ref[...])
    col_part = deposit(pick_cols, sums_back)
    scatter_col(0, col_part)
    spread_mat[...] = (
        lax.shift_right_logical(
            lax.broadcasted_iota(jnp.int32, spread_mat.shape, 0), SIDE.bit_length() - 1
        )
        == lax.broadcasted_iota(jnp.int32, spread_mat.shape, 1)
    ).astype(BF16)
    far_wait(0)

    @pl.when(diagonal)
    def _():
        far[0] = v_ref[...]

    theirs = fetch(pick_cols, far[0])
    block = v_ref[c].astype(F32)
    weighted = energy * block
    top = 2.0 * jnp.sum(theirs * sums_back, axis=0, keepdims=True) + jnp.sum(
        weighted * block, axis=0, keepdims=True
    )
    bottom = jnp.sum(block * block, axis=0, keepdims=True)
    lane = lax.broadcasted_iota(jnp.int32, num_out.shape, 1)
    odd = jnp.bitwise_and(lane, 1) == 1
    shift = SIDE // 2
    while shift:
        lower = jnp.bitwise_and(lane, shift) == 0
        top, bottom = (
            x + jnp.where(lower, pltpu.roll(x, width - shift, 1), pltpu.roll(x, shift, 1))
            for x in (top, bottom)
        )
        shift //= 2
    num_out[...] = jnp.where(odd, bottom, top)
    num_in[me] = num_out[...]
    each(1, everyone, lambda s: num_copy(s).start())

    scatter_row(0, deposit(pick_rows, forward(theirs)))
    def publish(phase, ref, block):
        parts = []
        for p in range(pairs):
            lanes = block[:, LANES * p: LANES * (p + 1)]
            parts.append((lanes[:half], lanes[half:]))
        for p in range(pairs):
            (turned,) = pack(list(parts[p]))
            for i in range(2):
                final[phase, pl.ds(2 * p + i, half, stride=here), :] = turned[i]
        lines(ref, c)[...] = final[phase]

    image = gathered(0, weighted)

    def num_step(s, carry):
        peer = lax.rem(me + s, everyone)
        copy(
            num_out, num_in.at[peer], num_send.at[0], num_recv.at[peer], r, c
        ).wait_recv()
        return carry

    lax.fori_loop(1, everyone, num_step, 0)
    sums = lax.fori_loop(
        0, everyone, lambda i, total: total + num_in[i], jnp.zeros(num_out.shape, F32)
    )
    after = pltpu.roll(sums, width - 1, 1)
    before = pltpu.roll(sums, 1, 1)
    theta = jnp.where(odd, before, sums) / jnp.where(odd, sums, after)
    residual = (image - theta * block).astype(BF16)
    near[c] = residual
    each(1, n, lambda s: far_copy(near.at[c], 1, s).start())
    each(1, n, lambda s: near_copy(s).start())

    def near_wait(s):
        q = lax.rem(c + s, n)
        copy(near.at[q], near.at[q], near_send.at[0], near_recv.at[q], r, c).wait_recv()

    publish(0, image_out, image)
    each(1, n, near_wait)
    each(1, n, lambda s: out_copy(0, image_out, s).start())
    scatter_col(1, deposit(pick_cols, backward(near[...])))
    far_wait(1)

    @pl.when(diagonal)
    def _():
        far[1] = near[...]

    scatter_row(1, deposit(pick_rows, forward(fetch(pick_cols, far[1]))))
    def out_wait(phase, ref, s):
        q = lax.rem(c + s, n)
        copy(
            final.at[phase], lines(ref, q), out_send.at[phase, 0], out_recv.at[phase, q], r, c
        ).wait_recv()

    def sent(s):
        out_copy(0, image_out, s).wait_send()
        row_copy(0, s).wait_send()
        far_copy(v_ref.at[c], 0, s).wait_send()
        far_copy(near.at[c], 1, s).wait_send()
        near_copy(s).wait_send()

    each(1, n, sent)
    for phase in range(2):
        each(0, n, lambda q: not_me(q, lambda: col_copy(phase, q).wait_send()))
    each(1, everyone, lambda s: num_copy(s).wait_send())
    each(1, n, lambda s: out_wait(0, image_out, s))
    publish(1, second_out, gathered(1, energy * residual.astype(F32)))
    each(1, n, lambda s: out_copy(1, second_out, s).start())

    def finish(s):
        out_wait(1, second_out, s)
        out_copy(1, second_out, s).wait_send()
        row_copy(1, s).wait_send()

    each(1, n, finish)


def store(image_ref, second_ref, image_out, second_out, sem):
    copies = [
        pltpu.make_async_copy(src, dst, sem.at[i])
        for i, (src, dst) in enumerate(((image_ref, image_out), (second_ref, second_out)))
    ]
    for move in copies:
        move.start()
    for move in copies:
        move.wait()


def local(n, vectors, energy, tiles, tile_rows, tile_cols, counts):
    here, group_width = vectors.shape
    groups = group_width // SIDE
    width = here * SIDE
    depth = groups // n
    slots, area = tiles.shape[2:]
    everyone = n * n
    pairs = width // LANES
    half_rows = groups // 2
    rows = here * half_rows
    vmem = pl.BlockSpec(memory_space=pltpu.VMEM)
    hbm = pl.BlockSpec(memory_space=pltpu.HBM)
    dma = pltpu.SemaphoreType.DMA
    image, second = pl.pallas_call(
        functools.partial(kernel, n),
        out_shape=[jax.ShapeDtypeStruct((rows, LANES), F32)] * 2,
        in_specs=[pl.BlockSpec(memory_space=pltpu.SMEM)] + [hbm] * 5,
        out_specs=[vmem, vmem],
        scratch_shapes=[
            pltpu.VMEM((rows, LANES), BF16),
            pltpu.VMEM((half_rows, LANES), F32),
            pltpu.VMEM((slots, area), BF16),
            pltpu.VMEM((1, slots), jnp.int32),
            pltpu.VMEM((1, slots), jnp.int32),
            pltpu.VMEM((n, depth, width), BF16),
            pltpu.VMEM((rows, LANES), F32),
            pltpu.VMEM((2, rows // n, LANES), F32),
            pltpu.VMEM((2 * area, LANES), BF16),
            pltpu.VMEM((LANES, area), BF16),
            pltpu.VMEM((LANES, area), BF16),
            pltpu.VMEM((pairs * slots, LANES), F32),
            pltpu.VMEM((2 * pairs, slots, LANES), F32),
            pltpu.VMEM((n, depth, width), BF16),
            pltpu.VMEM((2, n, depth, width), BF16),
            pltpu.VMEM((n, depth, width), F32),
            pltpu.VMEM((2, n, depth, width), BF16),
            pltpu.VMEM((2, n, depth, width), BF16),
            pltpu.VMEM((2, n, depth, width), BF16),
            pltpu.VMEM((2, n, depth, width), BF16),
            pltpu.VMEM((1, width), F32),
            pltpu.VMEM((everyone, 1, width), F32),
            dma((2, n)), dma((2, n)), dma((n,)), dma((n,)), dma((2, n)), dma((2, n)),
            dma((2, n)), dma((2, n)), dma((everyone,)), dma((everyone,)), dma((2, n)), dma((2, n)),
            dma((5,)),
        ],
        compiler_params=pltpu.CompilerParams(
            collective_id=0, has_side_effects=True, vmem_limit_bytes=32 * 1024 * 1024
        ),
    )(
        counts,
        *[
            pltpu.with_memory_space_constraint(x, pltpu.HBM)
            for x in (
                vectors.reshape(here, half_rows, LANES).transpose(1, 0, 2).reshape(rows, LANES),
                energy.reshape(half_rows, LANES), tile_rows[0], tile_cols[0], tiles[0, 0],
            )
        ]
    )

    image, second = pl.pallas_call(
        store,
        out_shape=[jax.ShapeDtypeStruct((rows, LANES), F32)] * 2,
        in_specs=[vmem] * 2,
        out_specs=[hbm] * 2,
        scratch_shapes=[dma((2,))],
        compiler_params=pltpu.CompilerParams(vmem_limit_bytes=4 * 1024 * 1024),
    )(image, second)

    def unfold(x):
        return x.reshape(half_rows, here, LANES).transpose(1, 0, 2).reshape(here, group_width)

    return unfold(image), unfold(second)


def solution(mesh):
    in_specs = (
        P("vec", "row"),
        P("row"),
        P("row", "col", None, None),
        P("row", "col", None),
        P("row", "col", None),
        P("row", "col"),
    )
    out_specs = (P("vec", "row"), P("vec", "row"))
    return jax.shard_map(
        functools.partial(local, mesh.shape["row"]), mesh=mesh, in_specs=in_specs,
        out_specs=out_specs, check_vma=False,
    )
```
